32 devices in a mesh: grp: 1, deg: 32 (over z, y, x, core).
Axes of the slice: x: 2, y: 2, z: 4, core: 2. Of those that a mesh axis runs over, the one named last changes fastest.
Arguments:
- coeffs_in: float32 [512, 1025, 128], P(('grp', 'deg')), may hold values from -6 to 6
- tables: bfloat16 [512, 1025, 1025], P('deg'), as said below
- order_pairs: int32 [512], replicated, may hold values from 0 to 511, each once
- degree_pairs: int32 [512], replicated, may hold values from 0 to 511, as said below
- angles: float32 [3], replicated, may hold values from -3.140625 to 3.140625
Outputs:
- coeffs_out: float32 [512, 1025, 128], P(('grp', 'deg'))
The draws below stay inside these ranges and needn't reach their ends.
Inputs may be any that keep to these rules, and one draw needn't show every extreme that they name: `order_pairs`: each pair of orders appears once. `degree_pairs`: each pair of degrees appears once. tables[j] is zero outside its two diagonal blocks: the first degree_pairs[j]+1 rows and columns, and the remaining 1024-degree_pairs[j].
All inputs are finite; a program needn't handle non-finite values.
Results may differ from the reference program's by a relative error of at most 0.005.
Values may be sent and summed in bfloat16 or wider, within the bound.
A program may use at most 192 MiB of HBM per device.

```python
import jax
import jax.numpy as jnp
from jax import lax

L = 1024
SH = 64
NPAIR = 512
WIDE = 1025


def pair_permutation(key):
    return jax.random.permutation(jax.random.fold_in(key, 11), NPAIR).astype(jnp.int32)


def draw_degree_pairs(key, part):
    return pair_permutation(key)


def draw_tables(key, part):
    pairs = pair_permutation(key)
    block_low = pairs[:, None, None] + 1
    row_index = jnp.arange(WIDE, dtype=jnp.int32)[None, :, None]
    col_index = jnp.arange(WIDE, dtype=jnp.int32)[None, None, :]
    upper_block = (row_index < block_low) & (col_index < block_low)
    lower_block = (row_index >= block_low) & (col_index >= block_low)
    block_size = jnp.where(row_index < block_low, block_low, WIDE - block_low).astype(jnp.float32)
    raw_values = jax.random.normal(jax.random.fold_in(key, 12), (NPAIR, WIDE, WIDE), jnp.float32)
    scaled = raw_values / jnp.sqrt(block_size)
    return jnp.where(upper_block | lower_block, scaled, 0.0).astype(jnp.bfloat16)


def level_of(stream_key, dims, split, smallest, high):
    gain = 1.0
    for dim, shards_of in split:
        draws = jax.random.uniform(jax.random.fold_in(jax.random.fold_in(stream_key, 6), dim), (shards_of,), jnp.float32, smallest / len(split), high / len(split))
        gain = gain * jnp.repeat(jnp.exp(draws), dims[dim] // shards_of).reshape((-1,) + (1,) * (len(dims) - 1 - dim))
    return gain


def bell_draw(stream_key, extent, deviation, most, cuts=(), kind=jnp.bfloat16):
    array = deviation * jax.random.normal(stream_key, extent, jnp.float32)
    if cuts:
        array = array * level_of(stream_key, extent, cuts, -0.22, 0.18)
    return jnp.clip(array, -most, most).astype(kind)


def setup_inputs(seed: int = 0, part: int = 0) -> dict:
    key_of = jax.random.split(jax.random.key(seed), 6)
    part_keys = jax.random.split(jax.random.fold_in(key_of[5], part), 6)
    coeffs_in = bell_draw(part_keys[0], (NPAIR, WIDE, 2 * SH), 1.0, 6.0, ((0, 32),), jnp.float32)
    tables = draw_tables(jax.random.fold_in(key_of[5], 71), part)
    order_pairs = jax.random.permutation(key_of[2], NPAIR).astype(jnp.int32)
    degree_pairs = draw_degree_pairs(jax.random.fold_in(key_of[5], 71), part)
    angles = jnp.clip(jax.random.uniform(key_of[4], (3,), jnp.float32, -3.140625, 3.140625), -3.140625, 3.140625)
    return dict(coeffs_in=coeffs_in, tables=tables, order_pairs=order_pairs, degree_pairs=degree_pairs, angles=angles)


def rotate_phase(values, order_map, angle):
    half = values.shape[-1] // 2
    turn = order_map.astype(jnp.float32)[..., None] * angle
    cosine = jnp.cos(turn)
    sine_part = jnp.sin(turn)
    real_part = values[..., :half].astype(jnp.float32)
    imag_part = values[..., half:].astype(jnp.float32)
    return jnp.concatenate([real_part * cosine + imag_part * sine_part, imag_part * cosine - real_part * sine_part], -1)


def reference(coeffs_in, tables, order_pairs, degree_pairs, angles):
    top = L
    position = jnp.arange(WIDE, dtype=jnp.int32)[None, :]
    order_low = order_pairs.astype(jnp.int32)[:, None]
    order_map = jnp.where(position < top - order_low, order_low, top - 1 - order_low)
    turned = rotate_phase(coeffs_in, order_map, angles[2]).astype(jnp.bfloat16)
    counting = jnp.arange(NPAIR, dtype=jnp.int32)
    inverse_order = jnp.zeros((NPAIR,), jnp.int32).at[order_pairs].set(counting)
    inverse_degree = jnp.zeros((NPAIR,), jnp.int32).at[degree_pairs].set(counting)
    degree_low = degree_pairs.astype(jnp.int32)[:, None]
    lower_part = position <= degree_low
    degree_full = jnp.where(lower_part, degree_low, top - 1 - degree_low)
    degree_map = jnp.where(lower_part, position, position - degree_low - 1)
    low_order = degree_map < NPAIR
    order_base = jnp.where(low_order, degree_map, top - 1 - degree_map)
    source_row = inverse_order[order_base]
    source_pos = jnp.where(low_order, degree_full - order_base, (top - order_base) + (degree_full - degree_map))
    by_degree = turned[source_row, source_pos]
    tilt = angles[1]

    def one_pair(packed):
        table, block, pair_orders = packed
        first_pass = jnp.dot(table, block, preferred_element_type=jnp.float32)
        tilted = rotate_phase(first_pass, pair_orders, tilt).astype(jnp.bfloat16)
        return jnp.dot(table, tilted, preferred_element_type=jnp.float32).astype(jnp.bfloat16)

    second = lax.map(one_pair, (tables, by_degree, degree_map))
    high_part = position >= top - order_low
    degree_back = jnp.where(high_part, position - 1, order_low + position)
    low_degree = degree_back < NPAIR
    pair_base = jnp.where(low_degree, degree_back, top - 1 - degree_back)
    target_pos = jnp.where(low_degree, order_map, pair_base + 1 + order_map)
    target_row = inverse_degree[pair_base]
    gathered = second[target_row, target_pos]
    return rotate_phase(gathered, order_map, angles[0])
```

```python
import functools

import jax
import jax.numpy as jnp
from jax import lax
from jax.experimental import pallas as pl
from jax.experimental.pallas import tpu as pltpu
from jax.sharding import PartitionSpec as P


def rotate_phase(values, order_map, angle):
    half = values.shape[-1] // 2
    turn = order_map.astype(jnp.float32)[..., None] * angle
    cosine = jnp.cos(turn)
    sine_part = jnp.sin(turn)
    real_part = values[..., :half].astype(jnp.float32)
    imag_part = values[..., half:].astype(jnp.float32)
    return jnp.concatenate(
        [real_part * cosine + imag_part * sine_part, imag_part * cosine - real_part * sine_part], -1
    )


def packed_places(order_low, degree_low, top):
    lower_side = order_low <= degree_low
    order_pos = jnp.stack(
        [
            top - 1 - degree_low - order_low,
            jnp.where(lower_side, degree_low - order_low, top - degree_low),
        ],
        -1,
    )
    degree_pos = jnp.stack(
        [
            degree_low + 1 + order_low,
            jnp.where(lower_side, order_low, top + degree_low - order_low),
        ],
        -1,
    )
    return (order_pos, degree_pos)


def indicator(places, alive, width):
    columns = jnp.arange(width, dtype=jnp.int32)
    return ((places[..., None] == columns) & alive[..., None]).astype(jnp.bfloat16)


def gather_slots(form, source, places, alive):
    width = source.shape[1]
    pieces = []
    for slot in range(places.shape[-1]):
        table = indicator(places[..., slot], alive[..., slot], width)
        pieces.append(
            jnp.einsum(form, table, source, preferred_element_type=jnp.float32).astype(jnp.bfloat16)
        )
    return jnp.stack(pieces, -2)


def place_slots(form, values, places, alive, width):
    total = None
    for slot in range(places.shape[-1]):
        table = indicator(places[..., slot], alive[..., slot], width)
        term = jnp.einsum(form, table, values[..., slot, :], preferred_element_type=jnp.float32)
        total = term if total is None else total + term
    return total.astype(jnp.bfloat16)


def transform(tables, by_degree, degree_map, tilt):
    first_pass = jnp.einsum("jab,jbc->jac", tables, by_degree, preferred_element_type=jnp.float32)
    tilted = rotate_phase(first_pass, degree_map, tilt).astype(jnp.bfloat16)
    second = jnp.einsum("jab,jbc->jac", tables, tilted, preferred_element_type=jnp.float32)
    return second.astype(jnp.bfloat16)


def small_shards(coeffs_in, tables, order_pairs, degree_pairs, angles):
    local_pairs, width, channels = coeffs_in.shape
    top = width - 1
    devices = lax.axis_size("deg")
    device = lax.axis_index("deg")
    my_orders = lax.dynamic_slice_in_dim(order_pairs, device * local_pairs, local_pairs)
    my_degrees = lax.dynamic_slice_in_dim(degree_pairs, device * local_pairs, local_pairs)
    all_orders = order_pairs.reshape(devices, local_pairs)
    all_degrees = degree_pairs.reshape(devices, local_pairs)
    position = jnp.arange(width, dtype=jnp.int32)[None, :]
    order_map = jnp.where(
        position < top - my_orders[:, None], my_orders[:, None], top - 1 - my_orders[:, None]
    )
    degree_map = jnp.where(
        position <= my_degrees[:, None], position, position - my_degrees[:, None] - 1
    )
    turned = rotate_phase(coeffs_in, order_map, angles[2]).astype(jnp.bfloat16)
    grid_shape = (devices, local_pairs, local_pairs)
    outward_orders = jnp.broadcast_to(my_orders[None, :, None], grid_shape)
    outward_degrees = jnp.broadcast_to(all_degrees[:, None, :], grid_shape)
    inward_orders = jnp.broadcast_to(all_orders[:, :, None], grid_shape)
    inward_degrees = jnp.broadcast_to(my_degrees[None, None, :], grid_shape)
    out_opos, out_dpos = packed_places(outward_orders, outward_degrees, top)
    in_opos, in_dpos = packed_places(inward_orders, inward_degrees, top)
    out_alive = jnp.ones(out_opos.shape, jnp.bool_)
    in_alive = jnp.ones(in_dpos.shape, jnp.bool_)
    out_found = jnp.any(outward_degrees == outward_orders, axis=-1)
    in_match = inward_degrees == inward_orders
    in_found = jnp.any(in_match, axis=-1)
    in_choice = jnp.argmax(in_match.astype(jnp.int32), axis=-1)
    degree_rows = jnp.arange(local_pairs, dtype=jnp.int32)
    matching = ((in_choice[..., None] == degree_rows) & in_found[..., None]).astype(jnp.bfloat16)
    row_found = jnp.any((in_choice[..., None] == degree_rows) & in_found[..., None], axis=(0, 1))
    extra_places = top - my_orders
    extra_values = jnp.take_along_axis(turned, extra_places[:, None, None], 1)[:, 0]
    main_send = gather_slots("drcw,rwx->drcx", turned, out_opos, out_alive)
    extra_send = jnp.where(out_found[..., None], extra_values[None], 0)
    main_arrived, extra_arrived = (
        lax.all_to_all(main_send, "deg", split_axis=0, concat_axis=0, tiled=True),
        lax.all_to_all(extra_send, "deg", split_axis=0, concat_axis=0, tiled=True),
    )
    by_degree = place_slots("drcw,drcx->cwx", main_arrived, in_dpos, in_alive, width)
    extra_column = jnp.einsum(
        "drq,drx->qx", matching, extra_arrived, preferred_element_type=jnp.float32
    ).astype(jnp.bfloat16)
    by_degree = by_degree.at[:, top].set(
        jnp.where(row_found[:, None], extra_column, by_degree[:, top])
    )
    second = transform(tables, by_degree, degree_map, angles[1])
    main_back = gather_slots("drcw,cwx->drcx", second, in_dpos, in_alive)
    extra_back = jnp.einsum(
        "drq,qx->drx", matching, second[:, top], preferred_element_type=jnp.float32
    ).astype(jnp.bfloat16)
    main_home, extra_home = (
        lax.all_to_all(main_back, "deg", split_axis=0, concat_axis=0, tiled=True),
        lax.all_to_all(extra_back, "deg", split_axis=0, concat_axis=0, tiled=True),
    )
    by_order = place_slots("drcw,drcx->rwx", main_home, out_opos, out_alive, width)
    home_values = jnp.sum(
        jnp.where(out_found[..., None], extra_home.astype(jnp.float32), 0.0), axis=0
    ).astype(jnp.bfloat16)
    home_found = jnp.any(out_found, axis=0)
    home_mask = (position == extra_places[:, None]) & home_found[:, None]
    by_order = jnp.where(home_mask[..., None], home_values[:, None, :], by_order)
    return rotate_phase(by_order, order_map, angles[0])


CHUNKS = 2
VMEM = pl.BlockSpec(memory_space=pltpu.VMEM)
SMEM = pl.BlockSpec(memory_space=pltpu.SMEM)
ANY = pl.BlockSpec(memory_space=pl.ANY)
F32 = jnp.float32
BF16 = jnp.bfloat16


def onehot(a, b):
    return jnp.where(a == b, 1.0, 0.0).astype(BF16)


def rotate(v, cosine, sine):
    return v * cosine + pltpu.roll(v, v.shape[-1] // 2, v.ndim - 1) * sine


def dot(a, b):
    return jnp.dot(a, b, preferred_element_type=F32)


def iota(shape, dim):
    return lax.broadcasted_iota(jnp.int32, shape, dim)


def pack_kernel(local, pairs, chunks, ord_ref, x_ref, qcol_ref, cs_ref, *rest):
    outs = rest[:chunks]
    xs, scr0, scr1, extra, q0, q1, sem = rest[chunks:]
    width = 2 * pairs + 1
    devices = pairs // local
    each = local // chunks
    copy = pltpu.make_async_copy(x_ref, xs.at[pl.ds(pairs * local, width * local)], sem)
    copy.start()
    column = iota((pairs, pairs), 1)
    q0[...] = onehot(column, pairs - 1 - qcol_ref[...])
    q1[...] = onehot(column, qcol_ref[...])
    copy.wait()
    row = iota((pairs, 1), 0)

    def step(r, carry):
        p = ord_ref[r]
        cl, sl, ch, sh = (cs_ref[i, pl.ds(r, 1), :] for i in range(4))

        def load(pos):
            return xs[pl.ds((pairs + pos) * local + r, pairs, stride=local), :]

        low = jnp.where(row >= p, rotate(load(-p), cl, sl), 0.0).astype(BF16)
        mid = rotate(load(pairs - p), cl, sl).astype(BF16)
        high = jnp.where(row >= pairs - p, rotate(load(pairs + 1), ch, sh), 0.0).astype(BF16)
        both = dot(q0[...], jnp.concatenate([mid, high], 1))
        scr0[pl.ds(r, pairs, stride=local), :] = both[:, :128]
        scr1[pl.ds(r, pairs, stride=local), :] = both[:, 128:] + dot(q1[...], low)
        extra[pl.ds(r, 1), :] = rotate(xs[pl.ds((pairs + width - 1 - p) * local + r, 1), :], ch, sh)
        return carry

    lax.fori_loop(0, local, step, 0)
    span = each * local

    def emit(d, carry):
        for k, out in enumerate(outs):
            at = pl.multiple_of(d * local * local + k * span, 16)
            out[d, 0:span, :] = scr0[pl.ds(at, span), :].astype(BF16)
            out[d, span : 2 * span, :] = scr1[pl.ds(at, span), :].astype(BF16)
        outs[0][d, 2 * span :, :] = extra[...].astype(BF16)
        return carry

    lax.fori_loop(0, devices, emit, 0)


def degree_kernel(local, pairs, each, last, deg_ref, recv, ein, eprev, prow, pcol, ct, st, table, *rest):
    if last:
        out, a0, arev, a0t, arevt, buf, eacc = rest
    else:
        out, eout, a0, arev, a0t, arevt, buf, eacc = rest
    width = 2 * pairs + 1
    devices = pairs // local
    c = pl.program_id(0)

    @pl.when(c == 0)
    def _():
        r0 = iota((pairs, pairs), 0)
        r1 = iota((pairs, pairs), 1)
        a0[...] = onehot(r0, prow[...])
        arev[...] = onehot(pairs - 1 - r0, prow[...])
        a0t[...] = onehot(r1, pcol[...])
        arevt[...] = onehot(pairs - 1 - r1, pcol[...])
        eacc[...] = eprev[...]

    q = deg_ref[c]
    at0 = pl.multiple_of(c * local, 16)
    at1 = pl.multiple_of((each + c) * local, 16)
    in0 = recv[:, pl.ds(at0, local), :].reshape(pairs, 128)
    in1 = recv[:, pl.ds(at1, local), :].reshape(pairs, 128)
    u = dot(a0[...], jnp.concatenate([in0, in1], 1))
    v = dot(arev[...], in1)
    pick = onehot(jnp.broadcast_to(prow[...], (8, pairs)), q)
    e = dot(pick, ein[...].reshape(pairs, 128))
    buf[0:pairs, :] = u[:, 128:]
    buf[pl.ds(q + 1, pairs), :] = u[:, :128]
    buf[pl.ds(q + 1 + pairs, pairs), :] = v
    buf[width - 1 : width, :] = e[0:1]
    first = dot(table[...], buf[0:width, :].astype(BF16))
    low = iota((width, 1), 0) <= q
    cosine = jnp.where(low, ct[pairs : pairs + width, :], ct[pl.ds(pairs - 1 - q, width), :])
    sine = jnp.where(low, st[pairs : pairs + width, :], st[pl.ds(pairs - 1 - q, width), :])
    tilted = rotate(first, cosine, sine).astype(BF16)
    buf[0:width, :] = dot(table[...], tilted).astype(BF16).astype(F32)
    row = iota((pairs, 1), 0)
    f0 = buf[pl.ds(q + 1, pairs), :].astype(BF16)
    f1 = jnp.where(row <= q, buf[0:pairs, :], 0.0).astype(BF16)
    back = jnp.where(row < pairs - 1 - q, buf[pl.ds(q + 1 + pairs, pairs), :], 0.0).astype(BF16)
    g = dot(a0t[...], jnp.concatenate([f0, f1], 1))
    h = g[:, 128:] + dot(arevt[...], back)
    out[:, pl.ds(at0, local), :] = g[:, :128].astype(BF16).reshape(devices, local, 128)
    out[:, pl.ds(at1, local), :] = h.astype(BF16).reshape(devices, local, 128)
    eacc[...] += jnp.where(pcol[...] == q, buf[width - 1 : width, :], 0.0)

    @pl.when(c == each - 1)
    def _():
        if last:
            out[:, 2 * each * local :, :] = eacc[...].astype(BF16).reshape(devices, local, 128)
        else:
            eout[...] = eacc[...]


def unpack_kernel(local, pairs, chunks, ord_ref, qrow_ref, cs_ref, *rest):
    backs = rest[:chunks]
    out_ref, os, scr0, scr1, extra, q0, q1, sem = rest[chunks:]
    width = 2 * pairs + 1
    devices = pairs // local
    each = local // chunks
    span = each * local
    extra[...] = jnp.zeros(extra.shape, F32)

    def take(d, carry):
        for k, back in enumerate(backs):
            at = pl.multiple_of(d * local * local + k * span, 16)
            scr0[pl.ds(at, span), :] = back[d, 0:span, :].astype(F32)
            scr1[pl.ds(at, span), :] = back[d, span : 2 * span, :].astype(F32)
        extra[...] += backs[-1][d, 2 * span :, :].astype(F32)
        return carry

    lax.fori_loop(0, devices, take, 0)
    row = iota((pairs, pairs), 0)
    q0[...] = onehot(pairs - 1 - row, qrow_ref[...])
    q1[...] = onehot(row, qrow_ref[...])

    def step(r, carry):
        p = ord_ref[r]
        cl, sl, ch, sh = (cs_ref[i, pl.ds(r, 1), :] for i in range(4))
        s0 = scr0[pl.ds(r, pairs, stride=local), :].astype(BF16)
        s1 = scr1[pl.ds(r, pairs, stride=local), :].astype(BF16)
        both = dot(q0[...], jnp.concatenate([s0, s1], 1))
        low = dot(q1[...], s1)

        def put(pos, value):
            os[pl.ds((pairs + pos) * local + r, pairs, stride=local), :] = value

        put(pairs + 1, rotate(both[:, 128:], ch, sh))
        put(-p, rotate(low, cl, sl))
        put(pairs - p, rotate(both[:, :128], cl, sl))
        os[pl.ds((pairs + width - 1 - p) * local + r, 1), :] = rotate(extra[pl.ds(r, 1), :], ch, sh)
        return carry

    lax.fori_loop(0, local, step, 0)
    copy = pltpu.make_async_copy(os.at[pl.ds(pairs * local, width * local)], out_ref, sem)
    copy.start()
    copy.wait()


def phases(orders, angle):
    turn = orders.astype(F32) * angle
    cosine, sine = jnp.cos(turn), jnp.sin(turn)
    lane = jnp.arange(128) < 64
    return (
        jnp.broadcast_to(cosine[:, None], (orders.shape[0], 128)),
        jnp.where(lane[None, :], sine[:, None], -sine[:, None]),
    )


def shards(coeffs_in, tables, order_pairs, degree_pairs, angles):
    local, width, channels = coeffs_in.shape
    top = width - 1
    pairs = top // 2
    if local % 16 or channels != 128 or pairs % 128:
        return small_shards(coeffs_in, tables, order_pairs, degree_pairs, angles)
    chunks = CHUNKS
    each = local // chunks
    devices = lax.axis_size("deg")
    device = lax.axis_index("deg")
    my_orders = lax.dynamic_slice_in_dim(order_pairs, device * local, local)
    my_degrees = lax.dynamic_slice_in_dim(degree_pairs, device * local, local)
    params = pltpu.CompilerParams(vmem_limit_bytes=56 * 1024 * 1024)
    turn_in = jnp.stack(phases(my_orders, angles[2]) + phases(top - 1 - my_orders, angles[2]))
    turn_out = jnp.stack(phases(my_orders, angles[0]) + phases(top - 1 - my_orders, angles[0]))
    ct, st = (
        jnp.pad(t, ((pairs, 7), (0, 0))) for t in phases(jnp.arange(width, dtype=jnp.int32), angles[1])
    )
    flat = jnp.transpose(coeffs_in, (1, 0, 2)).reshape(width * local, channels)
    main_rows = 2 * each * local
    rows = [main_rows + (local if k == 0 else 0) for k in range(chunks)]
    back_rows = [main_rows + (local if k == chunks - 1 else 0) for k in range(chunks)]
    square = pltpu.VMEM((pairs, pairs), BF16)
    slots = pltpu.VMEM((pairs * local, 128), F32)
    line = pltpu.VMEM(((pairs + width) * local, 128), F32)
    sends = pl.pallas_call(
        functools.partial(pack_kernel, local, pairs, chunks),
        name="pack",
        out_shape=[jax.ShapeDtypeStruct((devices, n, 128), BF16) for n in rows],
        in_specs=[SMEM, ANY, VMEM, VMEM],
        out_specs=[VMEM] * chunks,
        scratch_shapes=[line, slots, slots, pltpu.VMEM((local, 128), F32), square, square, pltpu.SemaphoreType.DMA],
        compiler_params=params,
        cost_estimate=pl.CostEstimate(flops=6 * 10**9, bytes_accessed=13 * 10**6, transcendentals=0),
    )(my_orders, flat, degree_pairs[:, None], turn_in)
    swap = functools.partial(lax.all_to_all, axis_name="deg", split_axis=0, concat_axis=0, tiled=True)
    arrived = [swap(s) for s in sends]
    extra_in = arrived[0][:, main_rows:, :]
    extra_back = jnp.zeros((pairs, 128), F32)
    homes = []
    for k in range(chunks):
        last = k == chunks - 1
        full2 = lambda c, deg: (0, 0)
        full3 = lambda c, deg: (0, 0, 0)
        out_shape = [jax.ShapeDtypeStruct((devices, back_rows[k], 128), BF16)]
        out_specs = [pl.BlockSpec((devices, back_rows[k], 128), full3)]
        if not last:
            out_shape.append(jax.ShapeDtypeStruct((pairs, 128), F32))
            out_specs.append(pl.BlockSpec((pairs, 128), full2))
        done = pl.pallas_call(
            functools.partial(degree_kernel, local, pairs, each, last),
            name="degree",
            out_shape=out_shape,
            grid_spec=pltpu.PrefetchScalarGridSpec(
                num_scalar_prefetch=1,
                grid=(each,),
                in_specs=[
                    pl.BlockSpec((devices, rows[k], 128), full3),
                    pl.BlockSpec((devices, local, 128), full3),
                    pl.BlockSpec((pairs, 128), full2),
                    pl.BlockSpec((1, pairs), full2),
                    pl.BlockSpec((pairs, 1), full2),
                    pl.BlockSpec(ct.shape, full2),
                    pl.BlockSpec(st.shape, full2),
                    pl.BlockSpec((None, width, width), lambda c, deg, k=k: (k * each + c, 0, 0)),
                ],
                out_specs=out_specs,
                scratch_shapes=[square] * 4
                + [pltpu.VMEM((3 * pairs + 16, 128), F32), pltpu.VMEM((pairs, 128), F32)],
            ),
            compiler_params=params,
            cost_estimate=pl.CostEstimate(
                flops=16 * 10**9 // chunks, bytes_accessed=50 * 10**6 // chunks, transcendentals=0
            ),
        )(
            my_degrees[k * each : (k + 1) * each], arrived[k], extra_in, extra_back,
            order_pairs[None, :], order_pairs[:, None], ct, st, tables,
        )
        if not last:
            extra_back = done[1]
        homes.append(swap(done[0]))
    result = pl.pallas_call(
        functools.partial(unpack_kernel, local, pairs, chunks),
        name="unpack",
        out_shape=jax.ShapeDtypeStruct((width * local, 128), F32),
        in_specs=[SMEM, VMEM, VMEM] + [VMEM] * chunks,
        out_specs=ANY,
        scratch_shapes=[line, slots, slots, pltpu.VMEM((local, 128), F32), square, square, pltpu.SemaphoreType.DMA],
        compiler_params=params,
        cost_estimate=pl.CostEstimate(flops=6 * 10**9, bytes_accessed=13 * 10**6, transcendentals=0),
    )(my_orders, degree_pairs[None, :], turn_out, *homes)
    return jnp.transpose(result.reshape(width, local, 128), (1, 0, 2))


def solution(mesh):
    return jax.shard_map(
        shards,
        mesh=mesh,
        in_specs=(P(("grp", "deg"), None, None), P("deg", None, None), P(), P(), P()),
        out_specs=P(("grp", "deg"), None, None),
        check_vma=False,
    )
```

```python
import functools

import jax
import jax.numpy as jnp
from jax import lax
from jax.experimental import pallas as pl
from jax.experimental.layout import Layout, with_layout_constraint
from jax.experimental.pallas import tpu as pltpu
from jax.sharding import PartitionSpec as P


def rotate_phase(values, order_map, angle):
    half = values.shape[-1] // 2
    turn = order_map.astype(jnp.float32)[..., None] * angle
    cosine = jnp.cos(turn)
    sine_part = jnp.sin(turn)
    real_part = values[..., :half].astype(jnp.float32)
    imag_part = values[..., half:].astype(jnp.float32)
    return jnp.concatenate(
        [real_part * cosine + imag_part * sine_part, imag_part * cosine - real_part * sine_part], -1
    )


def packed_places(order_low, degree_low, top):
    lower_side = order_low <= degree_low
    order_pos = jnp.stack(
        [
            top - 1 - degree_low - order_low,
            jnp.where(lower_side, degree_low - order_low, top - degree_low),
        ],
        -1,
    )
    degree_pos = jnp.stack(
        [
            degree_low + 1 + order_low,
            jnp.where(lower_side, order_low, top + degree_low - order_low),
        ],
        -1,
    )
    return (order_pos, degree_pos)


def indicator(places, alive, width):
    columns = jnp.arange(width, dtype=jnp.int32)
    return ((places[..., None] == columns) & alive[..., None]).astype(jnp.bfloat16)


def gather_slots(form, source, places, alive):
    width = source.shape[1]
    pieces = []
    for slot in range(places.shape[-1]):
        table = indicator(places[..., slot], alive[..., slot], width)
        pieces.append(
            jnp.einsum(form, table, source, preferred_element_type=jnp.float32).astype(jnp.bfloat16)
        )
    return jnp.stack(pieces, -2)


def place_slots(form, values, places, alive, width):
    total = None
    for slot in range(places.shape[-1]):
        table = indicator(places[..., slot], alive[..., slot], width)
        term = jnp.einsum(form, table, values[..., slot, :], preferred_element_type=jnp.float32)
        total = term if total is None else total + term
    return total.astype(jnp.bfloat16)


def transform(tables, by_degree, degree_map, tilt):
    first_pass = jnp.einsum("jab,jbc->jac", tables, by_degree, preferred_element_type=jnp.float32)
    tilted = rotate_phase(first_pass, degree_map, tilt).astype(jnp.bfloat16)
    second = jnp.einsum("jab,jbc->jac", tables, tilted, preferred_element_type=jnp.float32)
    return second.astype(jnp.bfloat16)


def small_shards(coeffs_in, tables, order_pairs, degree_pairs, angles):
    local_pairs, width, channels = coeffs_in.shape
    top = width - 1
    devices = lax.axis_size("deg")
    device = lax.axis_index("deg")
    my_orders = lax.dynamic_slice_in_dim(order_pairs, device * local_pairs, local_pairs)
    my_degrees = lax.dynamic_slice_in_dim(degree_pairs, device * local_pairs, local_pairs)
    all_orders = order_pairs.reshape(devices, local_pairs)
    all_degrees = degree_pairs.reshape(devices, local_pairs)
    position = jnp.arange(width, dtype=jnp.int32)[None, :]
    order_map = jnp.where(
        position < top - my_orders[:, None], my_orders[:, None], top - 1 - my_orders[:, None]
    )
    degree_map = jnp.where(
        position <= my_degrees[:, None], position, position - my_degrees[:, None] - 1
    )
    turned = rotate_phase(coeffs_in, order_map, angles[2]).astype(jnp.bfloat16)
    grid_shape = (devices, local_pairs, local_pairs)
    outward_orders = jnp.broadcast_to(my_orders[None, :, None], grid_shape)
    outward_degrees = jnp.broadcast_to(all_degrees[:, None, :], grid_shape)
    inward_orders = jnp.broadcast_to(all_orders[:, :, None], grid_shape)
    inward_degrees = jnp.broadcast_to(my_degrees[None, None, :], grid_shape)
    out_opos, out_dpos = packed_places(outward_orders, outward_degrees, top)
    in_opos, in_dpos = packed_places(inward_orders, inward_degrees, top)
    out_alive = jnp.ones(out_opos.shape, jnp.bool_)
    in_alive = jnp.ones(in_dpos.shape, jnp.bool_)
    out_found = jnp.any(outward_degrees == outward_orders, axis=-1)
    in_match = inward_degrees == inward_orders
    in_found = jnp.any(in_match, axis=-1)
    in_choice = jnp.argmax(in_match.astype(jnp.int32), axis=-1)
    degree_rows = jnp.arange(local_pairs, dtype=jnp.int32)
    matching = ((in_choice[..., None] == degree_rows) & in_found[..., None]).astype(jnp.bfloat16)
    row_found = jnp.any((in_choice[..., None] == degree_rows) & in_found[..., None], axis=(0, 1))
    extra_places = top - my_orders
    extra_values = jnp.take_along_axis(turned, extra_places[:, None, None], 1)[:, 0]
    main_send = gather_slots("drcw,rwx->drcx", turned, out_opos, out_alive)
    extra_send = jnp.where(out_found[..., None], extra_values[None], 0)
    main_arrived, extra_arrived = (
        lax.all_to_all(main_send, "deg", split_axis=0, concat_axis=0, tiled=True),
        lax.all_to_all(extra_send, "deg", split_axis=0, concat_axis=0, tiled=True),
    )
    by_degree = place_slots("drcw,drcx->cwx", main_arrived, in_dpos, in_alive, width)
    extra_column = jnp.einsum(
        "drq,drx->qx", matching, extra_arrived, preferred_element_type=jnp.float32
    ).astype(jnp.bfloat16)
    by_degree = by_degree.at[:, top].set(
        jnp.where(row_found[:, None], extra_column, by_degree[:, top])
    )
    second = transform(tables, by_degree, degree_map, angles[1])
    main_back = gather_slots("drcw,cwx->drcx", second, in_dpos, in_alive)
    extra_back = jnp.einsum(
        "drq,qx->drx", matching, second[:, top], preferred_element_type=jnp.float32
    ).astype(jnp.bfloat16)
    main_home, extra_home = (
        lax.all_to_all(main_back, "deg", split_axis=0, concat_axis=0, tiled=True),
        lax.all_to_all(extra_back, "deg", split_axis=0, concat_axis=0, tiled=True),
    )
    by_order = place_slots("drcw,drcx->rwx", main_home, out_opos, out_alive, width)
    home_values = jnp.sum(
        jnp.where(out_found[..., None], extra_home.astype(jnp.float32), 0.0), axis=0
    ).astype(jnp.bfloat16)
    home_found = jnp.any(out_found, axis=0)
    home_mask = (position == extra_places[:, None]) & home_found[:, None]
    by_order = jnp.where(home_mask[..., None], home_values[:, None, :], by_order)
    return rotate_phase(by_order, order_map, angles[0])


CHUNKS = 2
HALVES = 2
VMEM = pl.BlockSpec(memory_space=pltpu.VMEM)
SMEM = pl.BlockSpec(memory_space=pltpu.SMEM)
ANY = pl.BlockSpec(memory_space=pl.ANY)
F32 = jnp.float32
BF16 = jnp.bfloat16


def onehot(a, b):
    return jnp.where(a == b, 1.0, 0.0).astype(BF16)


def rotate(v, cosine, sine):
    return v * cosine + pltpu.roll(v, v.shape[-1] // 2, v.ndim - 1) * sine


def dot(a, b):
    return jnp.dot(a, b, preferred_element_type=F32)


def iota(shape, dim):
    return lax.broadcasted_iota(jnp.int32, shape, dim)


def pack_kernel(half, pairs, chunks, ord_ref, x_ref, qcol_ref, cs_ref, *rest):
    outs = rest[:chunks]
    xs3, scr0, scr1, extra, q0, q1, sem = rest[chunks:]
    part = cs_ref.shape[1]
    width = 2 * pairs + 1
    devices, each = outs[0].shape[0], outs[1].shape[1] // 2
    copy = pltpu.make_async_copy(
        x_ref.at[:, pl.ds(half * part, part), :], xs3.at[pl.ds(pairs, width)], sem
    )
    copy.start()
    xs = xs3.reshape((pairs + width) * part, 128)
    column = iota((pairs, pairs), 1)
    q0[...] = onehot(column, pairs - 1 - qcol_ref[...])
    q1[...] = onehot(column, qcol_ref[...])
    copy.wait()
    row = iota((pairs, 1), 0)

    def step(r, carry):
        p = ord_ref[r]
        cl, sl, ch, sh = (cs_ref[i, pl.ds(r, 1), :] for i in range(4))

        def load(pos):
            return xs[pl.ds((pairs + pos) * part + r, pairs, stride=part), :]

        low = jnp.where(row >= p, rotate(load(-p), cl, sl), 0.0).astype(BF16)
        mid = rotate(load(pairs - p), cl, sl).astype(BF16)
        high = jnp.where(row >= pairs - p, rotate(load(pairs + 1), ch, sh), 0.0).astype(BF16)
        both = dot(q0[...], jnp.concatenate([mid, high], 1))
        scr0[pl.ds(r, pairs, stride=part), :] = both[:, :128]
        scr1[pl.ds(r, pairs, stride=part), :] = both[:, 128:] + dot(q1[...], low)
        extra[pl.ds(r, 1), :] = rotate(xs[pl.ds((pairs + width - 1 - p) * part + r, 1), :], ch, sh)
        return carry

    lax.fori_loop(0, part, step, 0)
    span = each * part

    def emit(d, carry):
        for k, out in enumerate(outs):
            at = pl.multiple_of((d * chunks + k) * span, 8)
            out[d, 0:each] = scr0[pl.ds(at, span), :].reshape(each, part, 128).astype(BF16)
            out[d, each : 2 * each] = scr1[pl.ds(at, span), :].reshape(each, part, 128).astype(BF16)
        outs[0][d, 2 * each] = extra[...].astype(BF16)
        return carry

    lax.fori_loop(0, devices, emit, 0)


def degree_kernel(halves, pairs, each, last, deg_ref, *rest):
    joined = [h * 2 * each for h in range(halves)]
    count = 1 if last else halves
    recvs, rest = rest[:count], rest[count:]
    recvs = [(recvs[0], at) for at in joined] if last else [(ref, 0) for ref in recvs]
    eins, rest = [(ref, 0) for ref in rest[:halves]], rest[halves:]
    eprev, prow, pcol, ct, st, table = rest[:6]
    count = halves if last else 1
    outs, rest = rest[6 : 6 + count], rest[6 + count :]
    outs = [(ref, 0) for ref in outs] if last else [(outs[0], at) for at in joined]
    if not last:
        eout, rest = rest[0], rest[1:]
    a0, arev, a0t, arevt, buf, eacc = rest
    width = 2 * pairs + 1
    devices, part = recvs[0][0].shape[0], recvs[0][0].shape[2]
    size = devices * part
    c = pl.program_id(0)

    @pl.when(c == 0)
    def _():
        r0 = iota((pairs, pairs), 0)
        r1 = iota((pairs, pairs), 1)
        a0[...] = onehot(r0, prow[...])
        arev[...] = onehot(pairs - 1 - r0, prow[...])
        a0t[...] = onehot(r1, pcol[...])
        arevt[...] = onehot(pairs - 1 - r1, pcol[...])
        eacc[...] = eprev[...]

    def gather(refs, at):
        return jnp.concatenate(
            [ref[:, base + at].astype(F32).reshape(size, 128) for ref, base in refs], 0
        ).astype(BF16)

    def scatter(refs, at, value):
        for h, (ref, base) in enumerate(refs):
            ref[:, base + at] = value[h * size : (h + 1) * size].reshape(devices, part, 128).astype(BF16)

    q = deg_ref[c]
    in0 = gather(recvs, c)
    in1 = gather(recvs, each + c)
    u = dot(a0[...], jnp.concatenate([in0, in1], 1))
    v = dot(arev[...], in1)
    pick = onehot(jnp.broadcast_to(prow[...], (8, pairs)), q)
    e = dot(pick, gather(eins, 0))
    buf[0:pairs, :] = u[:, 128:]
    buf[pl.ds(q + 1, pairs), :] = u[:, :128]
    buf[pl.ds(q + 1 + pairs, pairs), :] = v
    buf[width - 1 : width, :] = e[0:1]
    first = dot(table[...], buf[0:width, :].astype(BF16))
    low = iota((width, 1), 0) <= q
    cosine = jnp.where(low, ct[pairs : pairs + width, :], ct[pl.ds(pairs - 1 - q, width), :])
    sine = jnp.where(low, st[pairs : pairs + width, :], st[pl.ds(pairs - 1 - q, width), :])
    tilted = rotate(first, cosine, sine).astype(BF16)
    buf[0:width, :] = dot(table[...], tilted).astype(BF16).astype(F32)
    row = iota((pairs, 1), 0)
    f0 = buf[pl.ds(q + 1, pairs), :].astype(BF16)
    f1 = jnp.where(row <= q, buf[0:pairs, :], 0.0).astype(BF16)
    back = jnp.where(row < pairs - 1 - q, buf[pl.ds(q + 1 + pairs, pairs), :], 0.0).astype(BF16)
    g = dot(a0t[...], jnp.concatenate([f0, f1], 1))
    scatter(outs, c, g[:, :128])
    scatter(outs, each + c, g[:, 128:] + dot(arevt[...], back))
    eacc[...] += jnp.where(pcol[...] == q, buf[width - 1 : width, :], 0.0)

    @pl.when(c == each - 1)
    def _():
        if last:
            scatter(outs, 2 * each, eacc[...])
        else:
            eout[...] = eacc[...]


def unpack_kernel(half, pairs, chunks, ord_ref, qrow_ref, cs_ref, *rest):
    backs = rest[:chunks]
    out_ref, os3, scr0, scr1, extra, q0, q1, sem = rest[-8:]
    part = cs_ref.shape[1]
    width = 2 * pairs + 1
    devices, each = backs[0].shape[0], backs[1].shape[1] // 2
    span = each * part
    os = os3.reshape((pairs + width) * part, 128)
    extra[...] = jnp.zeros(extra.shape, F32)

    def take(d, carry):
        for k, back in enumerate(backs):
            at = pl.multiple_of((d * chunks + k) * span, 8)
            base = half * 2 * each if k == 0 else 0
            scr0[pl.ds(at, span), :] = back[d, base : base + each].astype(F32).reshape(span, 128)
            scr1[pl.ds(at, span), :] = back[d, base + each : base + 2 * each].astype(F32).reshape(span, 128)
        extra[...] += backs[-1][d, 2 * each].astype(F32)
        return carry

    lax.fori_loop(0, devices, take, 0)
    row = iota((pairs, pairs), 0)
    q0[...] = onehot(pairs - 1 - row, qrow_ref[...])
    q1[...] = onehot(row, qrow_ref[...])

    def step(r, carry):
        p = ord_ref[r]
        cl, sl, ch, sh = (cs_ref[i, pl.ds(r, 1), :] for i in range(4))
        s0 = scr0[pl.ds(r, pairs, stride=part), :].astype(BF16)
        s1 = scr1[pl.ds(r, pairs, stride=part), :].astype(BF16)
        both = dot(q0[...], jnp.concatenate([s0, s1], 1))
        low = dot(q1[...], s1)

        def put(pos, value):
            os[pl.ds((pairs + pos) * part + r, pairs, stride=part), :] = value

        put(pairs + 1, rotate(both[:, 128:], ch, sh))
        put(-p, rotate(low, cl, sl))
        put(pairs - p, rotate(both[:, :128], cl, sl))
        os[pl.ds((pairs + width - 1 - p) * part + r, 1), :] = rotate(extra[pl.ds(r, 1), :], ch, sh)
        return carry

    lax.fori_loop(0, part, step, 0)
    copy = pltpu.make_async_copy(
        os3.at[pl.ds(pairs, width)], out_ref.at[:, pl.ds(half * part, part), :], sem
    )
    copy.start()
    copy.wait()


def phases(orders, angle):
    turn = orders.astype(F32) * angle
    cosine, sine = jnp.cos(turn), jnp.sin(turn)
    lane = jnp.arange(128) < 64
    return (
        jnp.broadcast_to(cosine[:, None], (orders.shape[0], 128)),
        jnp.where(lane[None, :], sine[:, None], -sine[:, None]),
    )


def shards(coeffs_in, tables, order_pairs, degree_pairs, angles):
    local, width, channels = coeffs_in.shape
    top = width - 1
    pairs = top // 2
    if local % 16 or channels != 128 or pairs % 128:
        return small_shards(coeffs_in, tables, order_pairs, degree_pairs, angles)
    chunks, halves = CHUNKS, HALVES
    each, part = local // chunks, local // halves
    devices = lax.axis_size("deg")
    device = lax.axis_index("deg")
    my_orders = lax.dynamic_slice_in_dim(order_pairs, device * local, local)
    my_degrees = lax.dynamic_slice_in_dim(degree_pairs, device * local, local)
    params = pltpu.CompilerParams(vmem_limit_bytes=56 * 1024 * 1024)
    cost = lambda flops, moved: pl.CostEstimate(flops=flops, bytes_accessed=moved, transcendentals=0)
    turn_in = jnp.stack(phases(my_orders, angles[2]) + phases(top - 1 - my_orders, angles[2]))
    turn_out = jnp.stack(phases(my_orders, angles[0]) + phases(top - 1 - my_orders, angles[0]))
    standing = jnp.transpose(coeffs_in, (1, 0, 2))
    rows = [2 * each + (k == 0) for k in range(chunks)]
    back_rows = [2 * each + (k == chunks - 1) for k in range(chunks)]
    square = pltpu.VMEM((pairs, pairs), BF16)
    slots = pltpu.VMEM((pairs * part, 128), F32)
    line = pltpu.VMEM((pairs + width, part, 128), F32)
    scratch = [line, slots, slots, pltpu.VMEM((part, 128), F32), square, square, pltpu.SemaphoreType.DMA]
    wire = lambda n: jax.ShapeDtypeStruct((devices, n, part, 128), BF16)
    mine = [my_orders[h * part : (h + 1) * part] for h in range(halves)]
    sends = [
        pl.pallas_call(
            functools.partial(pack_kernel, h, pairs, chunks),
            name="pack",
            out_shape=[wire(n) for n in rows],
            in_specs=[SMEM, ANY, VMEM, VMEM],
            out_specs=[VMEM] * chunks,
            scratch_shapes=scratch,
            compiler_params=params,
            cost_estimate=cost(6 * 10**9 // halves, 13 * 10**6 // halves),
        )(mine[h], standing, degree_pairs[:, None], turn_in[:, h * part : (h + 1) * part])
        for h in range(halves)
    ]
    swap = functools.partial(lax.all_to_all, axis_name="deg", split_axis=0, concat_axis=0, tiled=True)
    ct, st = (
        jnp.pad(t, ((pairs, 7), (0, 0))) for t in phases(jnp.arange(width, dtype=jnp.int32), angles[1])
    )
    by_part = jnp.transpose(order_pairs.reshape(devices, halves, part), (1, 0, 2)).reshape(-1)
    prow, pcol = by_part[None, :], by_part[:, None]
    tables = with_layout_constraint(tables, Layout((0, 1, 2)))
    arrived = [[swap(sends[h][0]) for h in range(halves)]]
    extra_in = [a[:, 2 * each :] for a in arrived[0]]
    later = jnp.concatenate([sends[h][1] for h in range(halves)], 1)
    later, tables, ct, st, pcol, extra_in = lax.optimization_barrier((later, tables, ct, st, pcol, extra_in))
    arrived.append([swap(later)])
    extra_back = jnp.zeros((pairs, 128), F32)
    homes = []
    for k in range(chunks):
        last = k == chunks - 1
        full = lambda shape: pl.BlockSpec(shape, lambda c, deg: (0,) * len(shape))
        out_shape = [wire(back_rows[k])] * halves if last else [wire(2 * each * halves)]
        out_specs = [full(w.shape) for w in out_shape]
        sent = len(out_shape)
        if not last:
            out_shape = out_shape + [jax.ShapeDtypeStruct((pairs, 128), F32)]
            out_specs = out_specs + [full((pairs, 128))]
        done = pl.pallas_call(
            functools.partial(degree_kernel, halves, pairs, each, last),
            name="degree",
            out_shape=out_shape,
            grid_spec=pltpu.PrefetchScalarGridSpec(
                num_scalar_prefetch=1,
                grid=(each,),
                in_specs=[full(a.shape) for a in arrived[k]]
                + [full((devices, 1, part, 128))] * halves
                + [full((pairs, 128)), full((1, pairs)), full((pairs, 1)), full(ct.shape), full(st.shape)]
                + [pl.BlockSpec((None, width, width), lambda c, deg, k=k: (k * each + c, 0, 0))],
                out_specs=out_specs,
                scratch_shapes=[square] * 4
                + [pltpu.VMEM((3 * pairs + 16, 128), F32), pltpu.VMEM((pairs, 128), F32)],
            ),
            compiler_params=params,
            cost_estimate=cost(16 * 10**9 // chunks, 50 * 10**6 // chunks),
        )(
            my_degrees[k * each : (k + 1) * each], *arrived[k], *extra_in,
            extra_back, prow, pcol, ct, st, tables,
        )
        if not last:
            extra_back = done[sent]
        homes.append([swap(d) for d in done[:sent]])
    result = ()
    for h in range(halves):
        result = (
            pl.pallas_call(
                functools.partial(unpack_kernel, h, pairs, chunks),
                name="unpack",
                out_shape=jax.ShapeDtypeStruct((width, local, 128), F32),
                in_specs=[SMEM, VMEM, VMEM] + [VMEM] * chunks + [ANY] * len(result),
                out_specs=ANY,
                scratch_shapes=scratch,
                input_output_aliases={3 + chunks: 0} if result else {},
                compiler_params=params,
                cost_estimate=cost(6 * 10**9 // halves, 13 * 10**6 // halves),
            )(
                mine[h], degree_pairs[None, :], turn_out[:, h * part : (h + 1) * part],
                homes[0][0], homes[1][h], *result,
            ),
        )
    return jnp.transpose(result[0], (1, 0, 2))


def solution(mesh):
    return jax.shard_map(
        shards,
        mesh=mesh,
        in_specs=(P(("grp", "deg"), None, None), P("deg", None, None), P(), P(), P()),
        out_specs=P(("grp", "deg"), None, None),
        check_vma=False,
    )
```

```python
import functools

import jax
import jax.numpy as jnp
from jax import lax
from jax.experimental import pallas as pl
from jax.experimental.layout import Layout, with_layout_constraint
from jax.experimental.pallas import tpu as pltpu
from jax.sharding import PartitionSpec as P


def rotate_phase(values, order_map, angle):
    half = values.shape[-1] // 2
    turn = order_map.astype(jnp.float32)[..., None] * angle
    cosine = jnp.cos(turn)
    sine_part = jnp.sin(turn)
    real_part = values[..., :half].astype(jnp.float32)
    imag_part = values[..., half:].astype(jnp.float32)
    return jnp.concatenate(
        [real_part * cosine + imag_part * sine_part, imag_part * cosine - real_part * sine_part], -1
    )


def packed_places(order_low, degree_low, top):
    lower_side = order_low <= degree_low
    order_pos = jnp.stack(
        [
            top - 1 - degree_low - order_low,
            jnp.where(lower_side, degree_low - order_low, top - degree_low),
        ],
        -1,
    )
    degree_pos = jnp.stack(
        [
            degree_low + 1 + order_low,
            jnp.where(lower_side, order_low, top + degree_low - order_low),
        ],
        -1,
    )
    return (order_pos, degree_pos)


def indicator(places, alive, width):
    columns = jnp.arange(width, dtype=jnp.int32)
    return ((places[..., None] == columns) & alive[..., None]).astype(jnp.bfloat16)


def gather_slots(form, source, places, alive):
    width = source.shape[1]
    pieces = []
    for slot in range(places.shape[-1]):
        table = indicator(places[..., slot], alive[..., slot], width)
        pieces.append(
            jnp.einsum(form, table, source, preferred_element_type=jnp.float32).astype(jnp.bfloat16)
        )
    return jnp.stack(pieces, -2)


def place_slots(form, values, places, alive, width):
    total = None
    for slot in range(places.shape[-1]):
        table = indicator(places[..., slot], alive[..., slot], width)
        term = jnp.einsum(form, table, values[..., slot, :], preferred_element_type=jnp.float32)
        total = term if total is None else total + term
    return total.astype(jnp.bfloat16)


def transform(tables, by_degree, degree_map, tilt):
    first_pass = jnp.einsum("jab,jbc->jac", tables, by_degree, preferred_element_type=jnp.float32)
    tilted = rotate_phase(first_pass, degree_map, tilt).astype(jnp.bfloat16)
    second = jnp.einsum("jab,jbc->jac", tables, tilted, preferred_element_type=jnp.float32)
    return second.astype(jnp.bfloat16)


def small_shards(coeffs_in, tables, order_pairs, degree_pairs, angles):
    local_pairs, width, channels = coeffs_in.shape
    top = width - 1
    devices = lax.axis_size("deg")
    device = lax.axis_index("deg")
    my_orders = lax.dynamic_slice_in_dim(order_pairs, device * local_pairs, local_pairs)
    my_degrees = lax.dynamic_slice_in_dim(degree_pairs, device * local_pairs, local_pairs)
    all_orders = order_pairs.reshape(devices, local_pairs)
    all_degrees = degree_pairs.reshape(devices, local_pairs)
    position = jnp.arange(width, dtype=jnp.int32)[None, :]
    order_map = jnp.where(
        position < top - my_orders[:, None], my_orders[:, None], top - 1 - my_orders[:, None]
    )
    degree_map = jnp.where(
        position <= my_degrees[:, None], position, position - my_degrees[:, None] - 1
    )
    turned = rotate_phase(coeffs_in, order_map, angles[2]).astype(jnp.bfloat16)
    grid_shape = (devices, local_pairs, local_pairs)
    outward_orders = jnp.broadcast_to(my_orders[None, :, None], grid_shape)
    outward_degrees = jnp.broadcast_to(all_degrees[:, None, :], grid_shape)
    inward_orders = jnp.broadcast_to(all_orders[:, :, None], grid_shape)
    inward_degrees = jnp.broadcast_to(my_degrees[None, None, :], grid_shape)
    out_opos, out_dpos = packed_places(outward_orders, outward_degrees, top)
    in_opos, in_dpos = packed_places(inward_orders, inward_degrees, top)
    out_alive = jnp.ones(out_opos.shape, jnp.bool_)
    in_alive = jnp.ones(in_dpos.shape, jnp.bool_)
    out_found = jnp.any(outward_degrees == outward_orders, axis=-1)
    in_match = inward_degrees == inward_orders
    in_found = jnp.any(in_match, axis=-1)
    in_choice = jnp.argmax(in_match.astype(jnp.int32), axis=-1)
    degree_rows = jnp.arange(local_pairs, dtype=jnp.int32)
    matching = ((in_choice[..., None] == degree_rows) & in_found[..., None]).astype(jnp.bfloat16)
    row_found = jnp.any((in_choice[..., None] == degree_rows) & in_found[..., None], axis=(0, 1))
    extra_places = top - my_orders
    extra_values = jnp.take_along_axis(turned, extra_places[:, None, None], 1)[:, 0]
    main_send = gather_slots("drcw,rwx->drcx", turned, out_opos, out_alive)
    extra_send = jnp.where(out_found[..., None], extra_values[None], 0)
    main_arrived, extra_arrived = (
        lax.all_to_all(main_send, "deg", split_axis=0, concat_axis=0, tiled=True),
        lax.all_to_all(extra_send, "deg", split_axis=0, concat_axis=0, tiled=True),
    )
    by_degree = place_slots("drcw,drcx->cwx", main_arrived, in_dpos, in_alive, width)
    extra_column = jnp.einsum(
        "drq,drx->qx", matching, extra_arrived, preferred_element_type=jnp.float32
    ).astype(jnp.bfloat16)
    by_degree = by_degree.at[:, top].set(
        jnp.where(row_found[:, None], extra_column, by_degree[:, top])
    )
    second = transform(tables, by_degree, degree_map, angles[1])
    main_back = gather_slots("drcw,cwx->drcx", second, in_dpos, in_alive)
    extra_back = jnp.einsum(
        "drq,qx->drx", matching, second[:, top], preferred_element_type=jnp.float32
    ).astype(jnp.bfloat16)
    main_home, extra_home = (
        lax.all_to_all(main_back, "deg", split_axis=0, concat_axis=0, tiled=True),
        lax.all_to_all(extra_back, "deg", split_axis=0, concat_axis=0, tiled=True),
    )
    by_order = place_slots("drcw,drcx->rwx", main_home, out_opos, out_alive, width)
    home_values = jnp.sum(
        jnp.where(out_found[..., None], extra_home.astype(jnp.float32), 0.0), axis=0
    ).astype(jnp.bfloat16)
    home_found = jnp.any(out_found, axis=0)
    home_mask = (position == extra_places[:, None]) & home_found[:, None]
    by_order = jnp.where(home_mask[..., None], home_values[:, None, :], by_order)
    return rotate_phase(by_order, order_map, angles[0])


CHUNKS = 2
HALVES = 2
VMEM = pl.BlockSpec(memory_space=pltpu.VMEM)
SMEM = pl.BlockSpec(memory_space=pltpu.SMEM)
ANY = pl.BlockSpec(memory_space=pl.ANY)
F32 = jnp.float32
BF16 = jnp.bfloat16


def onehot(a, b):
    return jnp.where(a == b, 1.0, 0.0).astype(BF16)


def rotate(v, cosine, sine):
    return v * cosine + pltpu.roll(v, v.shape[-1] // 2, v.ndim - 1) * sine


def dot(a, b):
    return jnp.dot(a, b, preferred_element_type=F32)


def iota(shape, dim):
    return lax.broadcasted_iota(jnp.int32, shape, dim)


def turning(orders, angle, top):
    rows = len(orders)
    shape = (rows, 128)
    low = jnp.zeros(shape, jnp.int32)
    for r, order in enumerate(orders):
        low = jnp.where(iota(shape, 0) == r, order, low)
    first = iota(shape, 1) < 64
    out = []
    for order in (low, top - 1 - low):
        turn = order.astype(F32) * angle
        sine = jnp.sin(turn)
        out += [jnp.cos(turn), jnp.where(first, sine, -sine)]
    return out


def pack_kernel(half, local, pairs, chunks, ord_ref, angle_ref, x_ref, qrow_ref, *rest):
    outs = rest[:chunks]
    xs3, scr0, scr1, extra, cs_ref, q0, q1, sem = rest[chunks:]
    part = xs3.shape[1]
    start = lax.axis_index("deg") * local + half * part
    width = 2 * pairs + 1
    devices, each = outs[0].shape[0], outs[1].shape[1] // 2
    copy = pltpu.make_async_copy(
        x_ref.at[:, pl.ds(half * part, part), :], xs3.at[pl.ds(pairs, width)], sem
    )
    copy.start()
    xs = xs3.reshape((pairs + width) * part, 128)
    level = iota((pairs, pairs), 0)
    q0[...] = jnp.where(pairs - 1 - level == qrow_ref[...], 1.0, 0.0).T.astype(BF16)
    q1[...] = jnp.where(level == qrow_ref[...], 1.0, 0.0).T.astype(BF16)
    for i, t in enumerate(turning([ord_ref[start + r] for r in range(part)], angle_ref[2], width - 1)):
        cs_ref[i] = t
    copy.wait()
    row = iota((pairs, 1), 0)

    def one(r):
        p = ord_ref[start + r]
        cl, sl, ch, sh = (cs_ref[i, pl.ds(r, 1), :] for i in range(4))

        def load(pos):
            return xs[pl.ds((pairs + pos) * part + r, pairs, stride=part), :]

        low = jnp.where(row >= p, rotate(load(-p), cl, sl), 0.0).astype(BF16)
        mid = rotate(load(pairs - p), cl, sl).astype(BF16)
        high = jnp.where(row >= pairs - p, rotate(load(pairs + 1), ch, sh), 0.0).astype(BF16)
        both = dot(q0[...], jnp.concatenate([mid, high], 1))
        extra[pl.ds(r, 1), :] = rotate(xs[pl.ds((pairs + width - 1 - p) * part + r, 1), :], ch, sh)
        return low, both

    def step(i, carry):
        r = 2 * i
        low_a, both_a = one(r)
        low_b, both_b = one(r + 1)
        lows = dot(q1[...], jnp.concatenate([low_a, low_b], 1))
        for at, both, low in ((r, both_a, lows[:, :128]), (r + 1, both_b, lows[:, 128:])):
            scr0[pl.ds(at, pairs, stride=part), :] = both[:, :128]
            scr1[pl.ds(at, pairs, stride=part), :] = both[:, 128:] + low
        return carry

    lax.fori_loop(0, part // 2, step, 0)
    span = each * part

    def emit(d, carry):
        for k, out in enumerate(outs):
            at = pl.multiple_of((d * chunks + k) * span, 8)
            out[d, 0:each] = scr0[pl.ds(at, span), :].reshape(each, part, 128).astype(BF16)
            out[d, each : 2 * each] = scr1[pl.ds(at, span), :].reshape(each, part, 128).astype(BF16)
        outs[0][d, 2 * each] = extra[...].astype(BF16)
        return carry

    lax.fori_loop(0, devices, emit, 0)


def degree_kernel(halves, pairs, each, last, deg_ref, *rest):
    joined = [h * 2 * each for h in range(halves)]
    count = 1 if last else halves
    recvs, rest = rest[:count], rest[count:]
    recvs = [(recvs[0], at) for at in joined] if last else [(ref, 0) for ref in recvs]
    eins, rest = [(ref, 0) for ref in rest[:halves]], rest[halves:]
    eprev, prow, pcol, ct, st, table = rest[:6]
    count = halves if last else 1
    outs, rest = rest[6 : 6 + count], rest[6 + count :]
    outs = [(ref, 0) for ref in outs] if last else [(outs[0], at) for at in joined]
    if not last:
        eout, rest = rest[0], rest[1:]
    a0, arev, a0t, arevt, buf, eacc = rest
    width = 2 * pairs + 1
    devices, part = recvs[0][0].shape[0], recvs[0][0].shape[2]
    size = devices * part
    c = pl.program_id(0)

    @pl.when(c == 0)
    def _():
        r0 = iota((pairs, pairs), 0)
        r1 = iota((pairs, pairs), 1)
        a0[...] = onehot(r0, prow[...])
        arev[...] = onehot(pairs - 1 - r0, prow[...])
        a0t[...] = onehot(r1, pcol[...])
        arevt[...] = onehot(pairs - 1 - r1, pcol[...])
        eacc[...] = eprev[...]

    def gather(refs, at):
        return jnp.concatenate(
            [ref[:, base + at].astype(F32).reshape(size, 128) for ref, base in refs], 0
        ).astype(BF16)

    def scatter(refs, at, value):
        for h, (ref, base) in enumerate(refs):
            ref[:, base + at] = value[h * size : (h + 1) * size].reshape(devices, part, 128).astype(BF16)

    q = deg_ref[c]
    in0 = gather(recvs, c)
    in1 = gather(recvs, each + c)
    u = dot(a0[...], jnp.concatenate([in0, in1], 1))
    v = dot(arev[...], in1)
    pick = onehot(jnp.broadcast_to(prow[...], (8, pairs)), q)
    e = dot(pick, gather(eins, 0))
    buf[0:pairs, :] = u[:, 128:]
    buf[pl.ds(q + 1, pairs), :] = u[:, :128]
    buf[pl.ds(q + 1 + pairs, pairs), :] = v
    buf[width - 1 : width, :] = e[0:1]
    first = dot(table[...], buf[0:width, :].astype(BF16))
    low = iota((width, 1), 0) <= q
    cosine = jnp.where(low, ct[pairs : pairs + width, :], ct[pl.ds(pairs - 1 - q, width), :])
    sine = jnp.where(low, st[pairs : pairs + width, :], st[pl.ds(pairs - 1 - q, width), :])
    tilted = rotate(first, cosine, sine).astype(BF16)
    buf[0:width, :] = dot(table[...], tilted).astype(BF16).astype(F32)
    row = iota((pairs, 1), 0)
    f0 = buf[pl.ds(q + 1, pairs), :].astype(BF16)
    f1 = jnp.where(row <= q, buf[0:pairs, :], 0.0).astype(BF16)
    back = jnp.where(row < pairs - 1 - q, buf[pl.ds(q + 1 + pairs, pairs), :], 0.0).astype(BF16)
    g = dot(a0t[...], jnp.concatenate([f0, f1], 1))
    scatter(outs, c, g[:, :128])
    scatter(outs, each + c, g[:, 128:] + dot(arevt[...], back))
    eacc[...] += jnp.where(pcol[...] == q, buf[width - 1 : width, :], 0.0)

    @pl.when(c == each - 1)
    def _():
        if last:
            scatter(outs, 2 * each, eacc[...])
        else:
            eout[...] = eacc[...]


def unpack_kernel(half, local, pairs, chunks, ord_ref, angle_ref, qrow_ref, *rest):
    backs = rest[:chunks]
    out_ref, os3, scr0, scr1, extra, cs_ref, q0, q1, sem = rest[-9:]
    part = os3.shape[1]
    start = lax.axis_index("deg") * local + half * part
    width = 2 * pairs + 1
    devices, each = backs[0].shape[0], backs[1].shape[1] // 2
    span = each * part
    os = os3.reshape((pairs + width) * part, 128)
    extra[...] = jnp.zeros(extra.shape, F32)

    def take(d, carry):
        for k, back in enumerate(backs):
            at = pl.multiple_of((d * chunks + k) * span, 8)
            base = half * 2 * each if k == 0 else 0
            scr0[pl.ds(at, span), :] = back[d, base : base + each].astype(F32).reshape(span, 128)
            scr1[pl.ds(at, span), :] = back[d, base + each : base + 2 * each].astype(F32).reshape(span, 128)
        extra[...] += backs[-1][d, 2 * each].astype(F32)
        return carry

    lax.fori_loop(0, devices, take, 0)
    row = iota((pairs, pairs), 0)
    q0[...] = onehot(pairs - 1 - row, qrow_ref[...])
    q1[...] = onehot(row, qrow_ref[...])
    for i, t in enumerate(turning([ord_ref[start + r] for r in range(part)], angle_ref[0], width - 1)):
        cs_ref[i] = t

    def step(i, carry):
        r = 2 * i
        s1s, boths = [], []
        for at in (r, r + 1):
            s0 = scr0[pl.ds(at, pairs, stride=part), :].astype(BF16)
            s1 = scr1[pl.ds(at, pairs, stride=part), :].astype(BF16)
            s1s.append(s1)
            boths.append(dot(q0[...], jnp.concatenate([s0, s1], 1)))
        lows = dot(q1[...], jnp.concatenate(s1s, 1))
        for at, both, low in ((r, boths[0], lows[:, :128]), (r + 1, boths[1], lows[:, 128:])):
            p = ord_ref[start + at]
            cl, sl, ch, sh = (cs_ref[i, pl.ds(at, 1), :] for i in range(4))

            def put(pos, value):
                os[pl.ds((pairs + pos) * part + at, pairs, stride=part), :] = value

            put(pairs + 1, rotate(both[:, 128:], ch, sh))
            put(-p, rotate(low, cl, sl))
            put(pairs - p, rotate(both[:, :128], cl, sl))
            os[pl.ds((pairs + width - 1 - p) * part + at, 1), :] = rotate(extra[pl.ds(at, 1), :], ch, sh)
        return carry

    lax.fori_loop(0, part // 2, step, 0)
    copy = pltpu.make_async_copy(
        os3.at[pl.ds(pairs, width)], out_ref.at[:, pl.ds(half * part, part), :], sem
    )
    copy.start()
    copy.wait()


def phases(orders, angle):
    turn = orders.astype(F32) * angle
    cosine, sine = jnp.cos(turn), jnp.sin(turn)
    lane = jnp.arange(128) < 64
    return (
        jnp.broadcast_to(cosine[:, None], (orders.shape[0], 128)),
        jnp.where(lane[None, :], sine[:, None], -sine[:, None]),
    )


def shards(coeffs_in, tables, order_pairs, degree_pairs, angles):
    local, width, channels = coeffs_in.shape
    top = width - 1
    pairs = top // 2
    if local % 16 or channels != 128 or pairs % 128:
        return small_shards(coeffs_in, tables, order_pairs, degree_pairs, angles)
    chunks, halves = CHUNKS, HALVES
    each, part = local // chunks, local // halves
    devices = lax.axis_size("deg")
    device = lax.axis_index("deg")
    my_degrees = lax.dynamic_slice_in_dim(degree_pairs, device * local, local)
    params = pltpu.CompilerParams(vmem_limit_bytes=56 * 1024 * 1024)
    cost = lambda flops, moved: pl.CostEstimate(flops=flops, bytes_accessed=moved, transcendentals=0)
    standing = jnp.transpose(coeffs_in, (1, 0, 2))
    rows = [2 * each + (k == 0) for k in range(chunks)]
    back_rows = [2 * each + (k == chunks - 1) for k in range(chunks)]
    square = pltpu.VMEM((pairs, pairs), BF16)
    slots = pltpu.VMEM((pairs * part, 128), F32)
    line = pltpu.VMEM((pairs + width, part, 128), F32)
    scratch = [line, slots, slots, pltpu.VMEM((part, 128), F32), pltpu.VMEM((4, part, 128), F32), square, square, pltpu.SemaphoreType.DMA]
    wire = lambda n: jax.ShapeDtypeStruct((devices, n, part, 128), BF16)
    sends = [
        pl.pallas_call(
            functools.partial(pack_kernel, h, local, pairs, chunks),
            name="pack",
            out_shape=[wire(n) for n in rows],
            in_specs=[SMEM, SMEM, ANY, VMEM],
            out_specs=[VMEM] * chunks,
            scratch_shapes=scratch,
            compiler_params=params,
            cost_estimate=cost(6 * 10**9 // halves, 13 * 10**6 // halves),
        )(order_pairs, angles, standing, degree_pairs[None, :])
        for h in range(halves)
    ]
    swap = functools.partial(lax.all_to_all, axis_name="deg", split_axis=0, concat_axis=0, tiled=True)
    ct, st = (
        jnp.pad(t, ((pairs, 7), (0, 0))) for t in phases(jnp.arange(width, dtype=jnp.int32), angles[1])
    )
    by_part = jnp.transpose(order_pairs.reshape(devices, halves, part), (1, 0, 2)).reshape(-1)
    prow, pcol = by_part[None, :], by_part[:, None]
    tabled = [
        with_layout_constraint(tables[k * each : (k + 1) * each], Layout((0, 1, 2))) for k in range(chunks)
    ]
    arrived = [[swap(sends[0][0])]]
    early, tabled[0], ct, st, prow, pcol = lax.optimization_barrier((sends[1][0], tabled[0], ct, st, prow, pcol))
    arrived[0].append(swap(early))
    extra_in = [a[:, 2 * each :] for a in arrived[0]]
    later = jnp.concatenate([sends[h][1] for h in range(halves)], 1)
    later, tabled[1], extra_in = lax.optimization_barrier((later, tabled[1], extra_in))
    arrived.append([swap(later)])
    extra_back = jnp.zeros((pairs, 128), F32)
    homes = []
    for k in range(chunks):
        last = k == chunks - 1
        full = lambda shape: pl.BlockSpec(shape, lambda c, deg: (0,) * len(shape))
        out_shape = [wire(back_rows[k])] * halves if last else [wire(2 * each * halves)]
        out_specs = [full(w.shape) for w in out_shape]
        sent = len(out_shape)
        if not last:
            out_shape = out_shape + [jax.ShapeDtypeStruct((pairs, 128), F32)]
            out_specs = out_specs + [full((pairs, 128))]
        done = pl.pallas_call(
            functools.partial(degree_kernel, halves, pairs, each, last),
            name="degree",
            out_shape=out_shape,
            grid_spec=pltpu.PrefetchScalarGridSpec(
                num_scalar_prefetch=1,
                grid=(each,),
                in_specs=[full(a.shape) for a in arrived[k]]
                + [full((devices, 1, part, 128))] * halves
                + [full((pairs, 128)), full((1, pairs)), full((pairs, 1)), full(ct.shape), full(st.shape)]
                + [pl.BlockSpec((None, width, width), lambda c, deg: (c, 0, 0))],
                out_specs=out_specs,
                scratch_shapes=[square] * 4
                + [pltpu.VMEM((3 * pairs + 16, 128), F32), pltpu.VMEM((pairs, 128), F32)],
            ),
            compiler_params=params,
            cost_estimate=cost(16 * 10**9 // chunks, 50 * 10**6 // chunks),
        )(
            my_degrees[k * each : (k + 1) * each], *arrived[k], *extra_in,
            extra_back, prow, pcol, ct, st, tabled[k],
        )
        if not last:
            extra_back = done[sent]
        homes.append([swap(d) for d in done[:sent]])
    result = ()
    for h in range(halves):
        result = (
            pl.pallas_call(
                functools.partial(unpack_kernel, h, local, pairs, chunks),
                name="unpack",
                out_shape=jax.ShapeDtypeStruct((width, local, 128), F32),
                in_specs=[SMEM, SMEM, VMEM] + [VMEM] * chunks + [ANY] * len(result),
                out_specs=ANY,
                scratch_shapes=scratch,
                input_output_aliases={3 + chunks: 0} if result else {},
                compiler_params=params,
                cost_estimate=cost(6 * 10**9 // halves, 13 * 10**6 // halves),
            )(
                order_pairs, angles, degree_pairs[None, :], homes[0][0], homes[1][h], *result,
            ),
        )
    return jnp.transpose(result[0], (1, 0, 2))


def solution(mesh):
    return jax.shard_map(
        shards,
        mesh=mesh,
        in_specs=(P(("grp", "deg"), None, None), P("deg", None, None), P(), P(), P()),
        out_specs=P(("grp", "deg"), None, None),
        check_vma=False,
    )
```

```python
import functools

import jax
import jax.numpy as jnp
from jax import lax
from jax.experimental import pallas as pl
from jax.experimental.layout import Layout, with_layout_constraint
from jax.experimental.pallas import tpu as pltpu
from jax.sharding import PartitionSpec as P


def rotate_phase(values, order_map, angle):
    half = values.shape[-1] // 2
    turn = order_map.astype(jnp.float32)[..., None] * angle
    cosine = jnp.cos(turn)
    sine_part = jnp.sin(turn)
    real_part = values[..., :half].astype(jnp.float32)
    imag_part = values[..., half:].astype(jnp.float32)
    return jnp.concatenate(
        [real_part * cosine + imag_part * sine_part, imag_part * cosine - real_part * sine_part], -1
    )


def packed_places(order_low, degree_low, top):
    lower_side = order_low <= degree_low
    order_pos = jnp.stack(
        [
            top - 1 - degree_low - order_low,
            jnp.where(lower_side, degree_low - order_low, top - degree_low),
        ],
        -1,
    )
    degree_pos = jnp.stack(
        [
            degree_low + 1 + order_low,
            jnp.where(lower_side, order_low, top + degree_low - order_low),
        ],
        -1,
    )
    return (order_pos, degree_pos)


def indicator(places, alive, width):
    columns = jnp.arange(width, dtype=jnp.int32)
    return ((places[..., None] == columns) & alive[..., None]).astype(jnp.bfloat16)


def gather_slots(form, source, places, alive):
    width = source.shape[1]
    pieces = []
    for slot in range(places.shape[-1]):
        table = indicator(places[..., slot], alive[..., slot], width)
        pieces.append(
            jnp.einsum(form, table, source, preferred_element_type=jnp.float32).astype(jnp.bfloat16)
        )
    return jnp.stack(pieces, -2)


def place_slots(form, values, places, alive, width):
    total = None
    for slot in range(places.shape[-1]):
        table = indicator(places[..., slot], alive[..., slot], width)
        term = jnp.einsum(form, table, values[..., slot, :], preferred_element_type=jnp.float32)
        total = term if total is None else total + term
    return total.astype(jnp.bfloat16)


def transform(tables, by_degree, degree_map, tilt):
    first_pass = jnp.einsum("jab,jbc->jac", tables, by_degree, preferred_element_type=jnp.float32)
    tilted = rotate_phase(first_pass, degree_map, tilt).astype(jnp.bfloat16)
    second = jnp.einsum("jab,jbc->jac", tables, tilted, preferred_element_type=jnp.float32)
    return second.astype(jnp.bfloat16)


def small_shards(coeffs_in, tables, order_pairs, degree_pairs, angles):
    local_pairs, width, channels = coeffs_in.shape
    top = width - 1
    devices = lax.axis_size("deg")
    device = lax.axis_index("deg")
    my_orders = lax.dynamic_slice_in_dim(order_pairs, device * local_pairs, local_pairs)
    my_degrees = lax.dynamic_slice_in_dim(degree_pairs, device * local_pairs, local_pairs)
    all_orders = order_pairs.reshape(devices, local_pairs)
    all_degrees = degree_pairs.reshape(devices, local_pairs)
    position = jnp.arange(width, dtype=jnp.int32)[None, :]
    order_map = jnp.where(
        position < top - my_orders[:, None], my_orders[:, None], top - 1 - my_orders[:, None]
    )
    degree_map = jnp.where(
        position <= my_degrees[:, None], position, position - my_degrees[:, None] - 1
    )
    turned = rotate_phase(coeffs_in, order_map, angles[2]).astype(jnp.bfloat16)
    grid_shape = (devices, local_pairs, local_pairs)
    outward_orders = jnp.broadcast_to(my_orders[None, :, None], grid_shape)
    outward_degrees = jnp.broadcast_to(all_degrees[:, None, :], grid_shape)
    inward_orders = jnp.broadcast_to(all_orders[:, :, None], grid_shape)
    inward_degrees = jnp.broadcast_to(my_degrees[None, None, :], grid_shape)
    out_opos, out_dpos = packed_places(outward_orders, outward_degrees, top)
    in_opos, in_dpos = packed_places(inward_orders, inward_degrees, top)
    out_alive = jnp.ones(out_opos.shape, jnp.bool_)
    in_alive = jnp.ones(in_dpos.shape, jnp.bool_)
    out_found = jnp.any(outward_degrees == outward_orders, axis=-1)
    in_match = inward_degrees == inward_orders
    in_found = jnp.any(in_match, axis=-1)
    in_choice = jnp.argmax(in_match.astype(jnp.int32), axis=-1)
    degree_rows = jnp.arange(local_pairs, dtype=jnp.int32)
    matching = ((in_choice[..., None] == degree_rows) & in_found[..., None]).astype(jnp.bfloat16)
    row_found = jnp.any((in_choice[..., None] == degree_rows) & in_found[..., None], axis=(0, 1))
    extra_places = top - my_orders
    extra_values = jnp.take_along_axis(turned, extra_places[:, None, None], 1)[:, 0]
    main_send = gather_slots("drcw,rwx->drcx", turned, out_opos, out_alive)
    extra_send = jnp.where(out_found[..., None], extra_values[None], 0)
    main_arrived, extra_arrived = (
        lax.all_to_all(main_send, "deg", split_axis=0, concat_axis=0, tiled=True),
        lax.all_to_all(extra_send, "deg", split_axis=0, concat_axis=0, tiled=True),
    )
    by_degree = place_slots("drcw,drcx->cwx", main_arrived, in_dpos, in_alive, width)
    extra_column = jnp.einsum(
        "drq,drx->qx", matching, extra_arrived, preferred_element_type=jnp.float32
    ).astype(jnp.bfloat16)
    by_degree = by_degree.at[:, top].set(
        jnp.where(row_found[:, None], extra_column, by_degree[:, top])
    )
    second = transform(tables, by_degree, degree_map, angles[1])
    main_back = gather_slots("drcw,cwx->drcx", second, in_dpos, in_alive)
    extra_back = jnp.einsum(
        "drq,qx->drx", matching, second[:, top], preferred_element_type=jnp.float32
    ).astype(jnp.bfloat16)
    main_home, extra_home = (
        lax.all_to_all(main_back, "deg", split_axis=0, concat_axis=0, tiled=True),
        lax.all_to_all(extra_back, "deg", split_axis=0, concat_axis=0, tiled=True),
    )
    by_order = place_slots("drcw,drcx->rwx", main_home, out_opos, out_alive, width)
    home_values = jnp.sum(
        jnp.where(out_found[..., None], extra_home.astype(jnp.float32), 0.0), axis=0
    ).astype(jnp.bfloat16)
    home_found = jnp.any(out_found, axis=0)
    home_mask = (position == extra_places[:, None]) & home_found[:, None]
    by_order = jnp.where(home_mask[..., None], home_values[:, None, :], by_order)
    return rotate_phase(by_order, order_map, angles[0])


CHUNKS = 2
HALVES = 2
VMEM = pl.BlockSpec(memory_space=pltpu.VMEM)
SMEM = pl.BlockSpec(memory_space=pltpu.SMEM)
ANY = pl.BlockSpec(memory_space=pl.ANY)
F32 = jnp.float32
BF16 = jnp.bfloat16


def onehot(a, b):
    return jnp.where(a == b, 1.0, 0.0).astype(BF16)


def rotate(v, cosine, sine):
    return v * cosine + pltpu.roll(v, v.shape[-1] // 2, v.ndim - 1) * sine


def dot(a, b):
    return jnp.dot(a, b, preferred_element_type=F32)


def iota(shape, dim):
    return lax.broadcasted_iota(jnp.int32, shape, dim)


def turning(orders, angle, top):
    rows = len(orders)
    shape = (rows, 128)
    low = jnp.zeros(shape, jnp.int32)
    for r, order in enumerate(orders):
        low = jnp.where(iota(shape, 0) == r, order, low)
    first = iota(shape, 1) < 64
    out = []
    for order in (low, top - 1 - low):
        turn = order.astype(F32) * angle
        sine = jnp.sin(turn)
        out += [jnp.cos(turn), jnp.where(first, sine, -sine)]
    return out


def pack_kernel(half, local, pairs, chunks, ord_ref, angle_ref, x_ref, qrow_ref, *rest):
    outs = rest[:chunks]
    xs3, scr0, scr1, extra, cs_ref, q0, q1, sem = rest[chunks:]
    part = xs3.shape[1]
    start = lax.axis_index("deg") * local + half * part
    width = 2 * pairs + 1
    devices, each = outs[0].shape[0], outs[1].shape[1] // 2
    copy = pltpu.make_async_copy(
        x_ref.at[:, pl.ds(half * part, part), :], xs3.at[pl.ds(pairs, width)], sem
    )
    copy.start()
    xs = xs3.reshape((pairs + width) * part, 128)
    level = iota((pairs, pairs), 0)
    q0[...] = jnp.where(pairs - 1 - level == qrow_ref[...], 1.0, 0.0).T.astype(BF16)
    q1[...] = jnp.where(level == qrow_ref[...], 1.0, 0.0).T.astype(BF16)
    for i, t in enumerate(turning([ord_ref[start + r] for r in range(part)], angle_ref[2], width - 1)):
        cs_ref[i] = t
    copy.wait()
    row = iota((pairs, 1), 0)

    def one(r):
        p = ord_ref[start + r]
        cl, sl, ch, sh = (cs_ref[i, pl.ds(r, 1), :] for i in range(4))

        def load(pos):
            return xs[pl.ds((pairs + pos) * part + r, pairs, stride=part), :]

        low = jnp.where(row >= p, rotate(load(-p), cl, sl), 0.0).astype(BF16)
        mid = rotate(load(pairs - p), cl, sl).astype(BF16)
        high = jnp.where(row >= pairs - p, rotate(load(pairs + 1), ch, sh), 0.0).astype(BF16)
        both = dot(q0[...], jnp.concatenate([mid, high], 1))
        extra[pl.ds(r, 1), :] = rotate(xs[pl.ds((pairs + width - 1 - p) * part + r, 1), :], ch, sh)
        return low, both

    def step(i, carry):
        r = 2 * i
        low_a, both_a = one(r)
        low_b, both_b = one(r + 1)
        lows = dot(q1[...], jnp.concatenate([low_a, low_b], 1))
        for at, both, low in ((r, both_a, lows[:, :128]), (r + 1, both_b, lows[:, 128:])):
            scr0[pl.ds(at, pairs, stride=part), :] = both[:, :128]
            scr1[pl.ds(at, pairs, stride=part), :] = both[:, 128:] + low
        return carry

    lax.fori_loop(0, part // 2, step, 0)
    span = each * part

    def emit(d, carry):
        for k, out in enumerate(outs):
            at = pl.multiple_of((d * chunks + k) * span, 8)
            out[d, 0:each] = scr0[pl.ds(at, span), :].reshape(each, part, 128).astype(BF16)
            out[d, each : 2 * each] = scr1[pl.ds(at, span), :].reshape(each, part, 128).astype(BF16)
        outs[0][d, 2 * each] = extra[...].astype(BF16)
        return carry

    lax.fori_loop(0, devices, emit, 0)


def degree_kernel(halves, pairs, each, last, deg_ref, *rest):
    joined = [h * 2 * each for h in range(halves)]
    count = 1 if last else halves
    recvs, rest = rest[:count], rest[count:]
    recvs = [(recvs[0], at) for at in joined] if last else [(ref, 0) for ref in recvs]
    eins, rest = [(ref, 0) for ref in rest[:halves]], rest[halves:]
    eprev, prow, pcol, ct, st, table = rest[:6]
    count = halves if last else 1
    outs, rest = rest[6 : 6 + count], rest[6 + count :]
    outs = [(ref, 0) for ref in outs] if last else [(outs[0], at) for at in joined]
    if not last:
        eout, rest = rest[0], rest[1:]
    a0, arev, a0t, arevt, buf, eacc = rest
    width = 2 * pairs + 1
    devices, part = recvs[0][0].shape[0], recvs[0][0].shape[2]
    size = devices * part
    c = pl.program_id(0)

    @pl.when(c == 0)
    def _():
        r0 = iota((pairs, pairs), 0)
        r1 = iota((pairs, pairs), 1)
        a0[...] = onehot(r0, prow[...])
        arev[...] = onehot(pairs - 1 - r0, prow[...])
        a0t[...] = onehot(r1, pcol[...])
        arevt[...] = onehot(pairs - 1 - r1, pcol[...])
        eacc[...] = eprev[...]

    def gather(refs, at):
        return jnp.concatenate(
            [ref[:, base + at].astype(F32).reshape(size, 128) for ref, base in refs], 0
        ).astype(BF16)

    def scatter(refs, at, value):
        for h, (ref, base) in enumerate(refs):
            ref[:, base + at] = value[h * size : (h + 1) * size].reshape(devices, part, 128).astype(BF16)

    q = deg_ref[c]
    in0 = gather(recvs, c)
    in1 = gather(recvs, each + c)
    u = dot(a0[...], jnp.concatenate([in0, in1], 1))
    v = dot(arev[...], in1)
    pick = onehot(jnp.broadcast_to(prow[...], (8, pairs)), q)
    e = dot(pick, gather(eins, 0))
    buf[0:pairs, :] = u[:, 128:]
    buf[pl.ds(q + 1, pairs), :] = u[:, :128]
    buf[pl.ds(q + 1 + pairs, pairs), :] = v
    buf[width - 1 : width, :] = e[0:1]
    first = dot(table[...], buf[0:width, :].astype(BF16))
    low = iota((width, 1), 0) <= q
    cosine = jnp.where(low, ct[pairs : pairs + width, :], ct[pl.ds(pairs - 1 - q, width), :])
    sine = jnp.where(low, st[pairs : pairs + width, :], st[pl.ds(pairs - 1 - q, width), :])
    tilted = rotate(first, cosine, sine).astype(BF16)
    buf[0:width, :] = dot(table[...], tilted).astype(BF16).astype(F32)
    row = iota((pairs, 1), 0)
    f0 = buf[pl.ds(q + 1, pairs), :].astype(BF16)
    f1 = jnp.where(row <= q, buf[0:pairs, :], 0.0).astype(BF16)
    back = jnp.where(row < pairs - 1 - q, buf[pl.ds(q + 1 + pairs, pairs), :], 0.0).astype(BF16)
    g = dot(a0t[...], jnp.concatenate([f0, f1], 1))
    scatter(outs, c, g[:, :128])
    scatter(outs, each + c, g[:, 128:] + dot(arevt[...], back))
    eacc[...] += jnp.where(pcol[...] == q, buf[width - 1 : width, :], 0.0)

    @pl.when(c == each - 1)
    def _():
        if last:
            scatter(outs, 2 * each, eacc[...])
        else:
            eout[...] = eacc[...]


def unpack_kernel(half, local, pairs, chunks, ord_ref, angle_ref, qrow_ref, *rest):
    backs = rest[:chunks]
    out_ref, os3, scr0, scr1, extra, cs_ref, q0, q1, sem = rest[-9:]
    part = os3.shape[1]
    start = lax.axis_index("deg") * local + half * part
    width = 2 * pairs + 1
    devices, each = backs[0].shape[0], backs[1].shape[1] // 2
    span = each * part
    os = os3.reshape((pairs + width) * part, 128)
    extra[...] = jnp.zeros(extra.shape, F32)

    def take(d, carry):
        for k, back in enumerate(backs):
            at = pl.multiple_of((d * chunks + k) * span, 8)
            base = half * 2 * each if k == 0 else 0
            scr0[pl.ds(at, span), :] = back[d, base : base + each].astype(F32).reshape(span, 128)
            scr1[pl.ds(at, span), :] = back[d, base + each : base + 2 * each].astype(F32).reshape(span, 128)
        extra[...] += backs[-1][d, 2 * each].astype(F32)
        return carry

    lax.fori_loop(0, devices, take, 0)
    row = iota((pairs, pairs), 0)
    q0[...] = onehot(pairs - 1 - row, qrow_ref[...])
    q1[...] = onehot(row, qrow_ref[...])
    for i, t in enumerate(turning([ord_ref[start + r] for r in range(part)], angle_ref[0], width - 1)):
        cs_ref[i] = t

    def step(i, carry):
        r = 2 * i
        s1s, boths = [], []
        for at in (r, r + 1):
            s0 = scr0[pl.ds(at, pairs, stride=part), :].astype(BF16)
            s1 = scr1[pl.ds(at, pairs, stride=part), :].astype(BF16)
            s1s.append(s1)
            boths.append(dot(q0[...], jnp.concatenate([s0, s1], 1)))
        lows = dot(q1[...], jnp.concatenate(s1s, 1))
        for at, both, low in ((r, boths[0], lows[:, :128]), (r + 1, boths[1], lows[:, 128:])):
            p = ord_ref[start + at]
            cl, sl, ch, sh = (cs_ref[i, pl.ds(at, 1), :] for i in range(4))

            def put(pos, value):
                os[pl.ds((pairs + pos) * part + at, pairs, stride=part), :] = value

            put(pairs + 1, rotate(both[:, 128:], ch, sh))
            put(-p, rotate(low, cl, sl))
            put(pairs - p, rotate(both[:, :128], cl, sl))
            os[pl.ds((pairs + width - 1 - p) * part + at, 1), :] = rotate(extra[pl.ds(at, 1), :], ch, sh)
        return carry

    lax.fori_loop(0, part // 2, step, 0)
    copy = pltpu.make_async_copy(
        os3.at[pl.ds(pairs, width)], out_ref.at[:, pl.ds(half * part, part), :], sem
    )
    copy.start()
    copy.wait()


def phases(orders, angle):
    turn = orders.astype(F32) * angle
    cosine, sine = jnp.cos(turn), jnp.sin(turn)
    lane = jnp.arange(128) < 64
    return (
        jnp.broadcast_to(cosine[:, None], (orders.shape[0], 128)),
        jnp.where(lane[None, :], sine[:, None], -sine[:, None]),
    )


def shards(coeffs_in, tables, order_pairs, degree_pairs, angles):
    local, width, channels = coeffs_in.shape
    top = width - 1
    pairs = top // 2
    if local % 16 or channels != 128 or pairs % 128:
        return small_shards(coeffs_in, tables, order_pairs, degree_pairs, angles)
    chunks, halves = CHUNKS, HALVES
    each, part = local // chunks, local // halves
    devices = lax.axis_size("deg")
    device = lax.axis_index("deg")
    my_degrees = lax.dynamic_slice_in_dim(degree_pairs, device * local, local)
    params = pltpu.CompilerParams(vmem_limit_bytes=56 * 1024 * 1024)
    cost = lambda flops, moved: pl.CostEstimate(flops=flops, bytes_accessed=moved, transcendentals=0)
    standing = jnp.transpose(coeffs_in, (1, 0, 2))
    rows = [2 * each + (k == 0) for k in range(chunks)]
    back_rows = [2 * each + (k == chunks - 1) for k in range(chunks)]
    square = pltpu.VMEM((pairs, pairs), BF16)
    slots = pltpu.VMEM((pairs * part, 128), F32)
    line = pltpu.VMEM((pairs + width, part, 128), F32)
    scratch = [line, slots, slots, pltpu.VMEM((part, 128), F32), pltpu.VMEM((4, part, 128), F32), square, square, pltpu.SemaphoreType.DMA]
    wire = lambda n: jax.ShapeDtypeStruct((devices, n, part, 128), BF16)
    sends = [
        pl.pallas_call(
            functools.partial(pack_kernel, h, local, pairs, chunks),
            name="pack",
            out_shape=[wire(n) for n in rows],
            in_specs=[SMEM, SMEM, ANY, VMEM],
            out_specs=[VMEM] * chunks,
            scratch_shapes=scratch,
            compiler_params=params,
            cost_estimate=cost(6 * 10**9 // halves, 13 * 10**6 // halves),
        )(order_pairs, angles, standing, degree_pairs[None, :])
        for h in range(halves)
    ]
    swap = functools.partial(lax.all_to_all, axis_name="deg", split_axis=0, concat_axis=0, tiled=True)
    first, tilt, sorted_orders = lax.optimization_barrier((sends[0][0], angles[1], order_pairs))
    ct, st = (
        jnp.pad(t, ((pairs, 7), (0, 0))) for t in phases(jnp.arange(width, dtype=jnp.int32), tilt)
    )
    by_part = jnp.transpose(sorted_orders.reshape(devices, halves, part), (1, 0, 2)).reshape(-1)
    prow, pcol = by_part[None, :], by_part[:, None]
    tables = with_layout_constraint(tables, Layout((0, 1, 2)))
    arrived = [[swap(first)]]
    early, ct, st, prow, pcol = lax.optimization_barrier((sends[1][0], ct, st, prow, pcol))
    arrived[0].append(swap(early))
    extra_in = [a[:, 2 * each :] for a in arrived[0]]
    later = jnp.concatenate([sends[h][1] for h in range(halves)], 1)
    later, tables, extra_in = lax.optimization_barrier((later, tables, extra_in))
    arrived.append([swap(later)])
    extra_back = jnp.zeros((pairs, 128), F32)
    homes = []
    for k in range(chunks):
        last = k == chunks - 1
        full = lambda shape: pl.BlockSpec(shape, lambda c, deg: (0,) * len(shape))
        out_shape = [wire(back_rows[k])] * halves if last else [wire(2 * each * halves)]
        out_specs = [full(w.shape) for w in out_shape]
        sent = len(out_shape)
        if not last:
            out_shape = out_shape + [jax.ShapeDtypeStruct((pairs, 128), F32)]
            out_specs = out_specs + [full((pairs, 128))]
        done = pl.pallas_call(
            functools.partial(degree_kernel, halves, pairs, each, last),
            name="degree",
            out_shape=out_shape,
            grid_spec=pltpu.PrefetchScalarGridSpec(
                num_scalar_prefetch=1,
                grid=(each,),
                in_specs=[full(a.shape) for a in arrived[k]]
                + [full((devices, 1, part, 128))] * halves
                + [full((pairs, 128)), full((1, pairs)), full((pairs, 1)), full(ct.shape), full(st.shape)]
                + [pl.BlockSpec((None, width, width), lambda c, deg, k=k: (k * each + c, 0, 0))],
                out_specs=out_specs,
                scratch_shapes=[square] * 4
                + [pltpu.VMEM((3 * pairs + 16, 128), F32), pltpu.VMEM((pairs, 128), F32)],
            ),
            compiler_params=params,
            cost_estimate=cost(16 * 10**9 // chunks, 50 * 10**6 // chunks),
        )(
            my_degrees[k * each : (k + 1) * each], *arrived[k], *extra_in,
            extra_back, prow, pcol, ct, st, tables,
        )
        if not last:
            extra_back = done[sent]
        homes.append([swap(d) for d in done[:sent]])
    result = ()
    for h in range(halves):
        result = (
            pl.pallas_call(
                functools.partial(unpack_kernel, h, local, pairs, chunks),
                name="unpack",
                out_shape=jax.ShapeDtypeStruct((width, local, 128), F32),
                in_specs=[SMEM, SMEM, VMEM] + [VMEM] * chunks + [ANY] * len(result),
                out_specs=ANY,
                scratch_shapes=scratch,
                input_output_aliases={3 + chunks: 0} if result else {},
                compiler_params=params,
                cost_estimate=cost(6 * 10**9 // halves, 13 * 10**6 // halves),
            )(
                order_pairs, angles, degree_pairs[None, :], homes[0][0], homes[1][h], *result,
            ),
        )
    return jnp.transpose(result[0], (1, 0, 2))


def solution(mesh):
    return jax.shard_map(
        shards,
        mesh=mesh,
        in_specs=(P(("grp", "deg"), None, None), P("deg", None, None), P(), P(), P()),
        out_specs=P(("grp", "deg"), None, None),
        check_vma=False,
    )
```
